1024 devices in a mesh: ctx: 128 (over z, y), head: 8 (over x, core).
Axes of the slice: x: 4, y: 4, z: 32, core: 2. Of those that a mesh axis runs over, the one named last changes fastest.
Arguments:
- query_self: bfloat16 [8192, 8192], P('ctx', 'head'), may hold values from -60 to 60
- key_self: bfloat16 [8192, 1024], P('ctx', 'head'), may hold values from -6 to 6
- value_self: bfloat16 [8192, 1024], P('ctx', 'head'), may hold values from -6 to 6
- positions: int32 [8192], P('ctx'), may hold values from 0 to 24573, as said below
- query_cross: bfloat16 [8192, 8192], P('ctx', 'head'), may hold values from -60 to 60
- key_vision: bfloat16 [7168, 1024], P('ctx', 'head'), may hold values from -6 to 6
- value_vision: bfloat16 [7168, 1024], P('ctx', 'head'), may hold values from -6 to 6
- media_range: int32 [512, 2], P('ctx'), may hold values from 0 to 8, as said below
- gate_scale: float32 [1], replicated, may hold values from 0.3 to 1.5
Outputs:
- self_context: bfloat16 [8192, 8192], P(('ctx', 'head'))
- cross_context: bfloat16 [8192, 8192], P(('ctx', 'head'))
The draws below stay inside these ranges and needn't reach their ends.
Inputs may be any that keep to these rules, and one draw needn't show every extreme that they name: `positions`: strictly increasing along the transcript, starting at 0; gaps of 1 to 3 up to the next-to-last token, and the last token's position is exactly 24573. `media_range`: column 0 never exceeds column 1; column 1 never falls from block to block, is 0 for the leading blocks (which see no frame) and 8 for the last block.
All inputs are finite; a program needn't handle non-finite values.
Results may differ from the reference program's by a relative error of at most 0.0091.
Values may be sent and summed in bfloat16 or wider, within the bound.
A program may use at most 32 MiB of HBM per device.

```python
import jax
import jax.numpy as jnp
from jax import lax

HQ = 64
KVH = 8
HD = 128
TBLOCK = 16
FRAMES = 8
FRAME_LEN = 896
TEXT = 8192
BLOCKS = 512
VIS = 7168


def media_table(key):
    inner_key = jax.random.fold_in(key, 55)
    bump_draw = jax.random.randint(jax.random.fold_in(inner_key, 1), (BLOCKS,), 0, 2)
    block_index = jnp.arange(BLOCKS, dtype=jnp.int32)
    upper_frame = jnp.clip(block_index * (FRAMES + 1) // BLOCKS - 1 + bump_draw, 0, FRAMES)
    upper_frame = lax.cummax(upper_frame, axis=0)
    upper_frame = upper_frame.at[BLOCKS - 1].set(FRAMES)
    reach_frames = jax.random.randint(jax.random.fold_in(inner_key, 2), (BLOCKS,), 1, FRAMES + 1)
    lower_frame = jnp.maximum(upper_frame - reach_frames, 0)
    return jnp.stack([lower_frame, upper_frame], axis=1).astype(jnp.int32)


def base_draw(key, salt, shape, scale):
    return jnp.clip(scale * jax.random.normal(jax.random.fold_in(key, salt), shape, jnp.float32), -6.0 * scale, 6.0 * scale)


def draw_query_self(key, part):
    drawn = base_draw(key, 11, (TEXT, HQ * HD), 2.5)
    return drawn.astype(jnp.bfloat16)


def draw_key_self(key, part):
    drawn = base_draw(key, 12, (TEXT, KVH * HD), 1.0)
    return drawn.astype(jnp.bfloat16)


def draw_positions(key, part):
    gaps = jax.random.randint(jax.random.fold_in(key, 21), (TEXT,), 1, 4)
    running = jnp.cumsum(gaps)
    running = running - running[0]
    running = running.at[TEXT - 1].set(3 * (TEXT - 1))
    return running.astype(jnp.int32)


def draw_query_cross(key, part):
    drawn = base_draw(key, 14, (TEXT, HQ * HD), 2.5)
    return drawn.astype(jnp.bfloat16)


def draw_key_vision(key, part):
    drawn = base_draw(key, 13, (VIS, KVH * HD), 1.0)
    return drawn.astype(jnp.bfloat16)


def draw_media_range(key, part):
    return media_table(key)


def steps_of(key, shape, cuts, low, high):
    def one(dim, shards_of):
        steps = jax.random.uniform(jax.random.fold_in(jax.random.fold_in(key, 6), dim), (shards_of,), jnp.float32, low / len(cuts), high / len(cuts))
        return jnp.repeat(jnp.exp(steps), shape[dim] // shards_of).reshape((-1,) + (1,) * (len(shape) - dim - 1))

    gain = one(*cuts[0])
    for cut in cuts[1:]:
        gain = gain * one(*cut)
    return gain


def noise(stream_key, shape, deviation, reach, split=(), held_as=jnp.bfloat16):
    array = jax.random.normal(stream_key, shape, jnp.float32) * deviation
    if len(split) > 0:
        array = steps_of(stream_key, shape, split, -0.22, 0.18) * array
    return jnp.clip(array, min=-reach, max=reach).astype(held_as)


def setup_inputs(seed: int = 0) -> dict:
    splits = jax.random.split(jax.random.key(seed), 10)
    return {
        "query_self": draw_query_self(jax.random.fold_in(splits[9], 71), 0),
        "key_self": draw_key_self(jax.random.fold_in(splits[9], 71), 0),
        "value_self": noise(splits[2], (TEXT, KVH * HD), 1.0, 6.0, ((0, 128), (1, 8))),
        "positions": draw_positions(jax.random.fold_in(splits[9], 71), 0),
        "query_cross": draw_query_cross(jax.random.fold_in(splits[9], 71), 0),
        "key_vision": draw_key_vision(jax.random.fold_in(splits[9], 71), 0),
        "value_vision": noise(splits[6], (VIS, KVH * HD), 1.0, 6.0, ((0, 128), (1, 8))),
        "media_range": draw_media_range(jax.random.fold_in(splits[9], 71), 0),
        "gate_scale": jnp.clip(jax.random.uniform(splits[8], (1,), jnp.float32, 0.3, 1.5), 0.3, 1.5),
    }


rope_base = 500000.0
lowest = -1e30


def rotate(values, positions):
    half_width = values.shape[-1] // 2
    exponents = jnp.arange(half_width, dtype=jnp.float32) * (2.0 / values.shape[-1])
    frequency = jnp.power(rope_base, -exponents)
    angles = positions.astype(jnp.float32)[:, None] * frequency[None, :]
    cosine = jnp.cos(angles)[:, None, :]
    sine_part = jnp.sin(angles)[:, None, :]
    first_half = values[..., :half_width]
    second_half = values[..., half_width:]
    return jnp.concatenate([first_half * cosine - second_half * sine_part, second_half * cosine + first_half * sine_part], axis=-1)


def blocked(queries, key_rows, value_rows, mask_rows):
    total_rows = queries.shape[0]
    group_size = queries.shape[2]
    block_rows = 512 if total_rows % 512 == 0 else total_rows
    block_count = total_rows // block_rows
    scale_factor = HD ** -0.5

    def one_block(item_index):
        head_index = item_index // block_count
        row_begin = (item_index % block_count) * block_rows
        query_block = lax.dynamic_slice_in_dim(queries, row_begin, block_rows, 0)
        query_block = lax.dynamic_index_in_dim(query_block, head_index, 1, keepdims=False)
        key_part = lax.dynamic_index_in_dim(key_rows, head_index, 1, keepdims=False)
        value_part = lax.dynamic_index_in_dim(value_rows, head_index, 1, keepdims=False)
        allowed = mask_rows(row_begin, block_rows)[None, :, :]
        scores = jnp.einsum("rgd,md->grm", query_block.astype(jnp.float32), key_part.astype(jnp.float32)) * scale_factor
        scores = jnp.where(allowed, scores, lowest)
        row_peak = jnp.max(scores, axis=-1, keepdims=True)
        weights = jnp.where(allowed, jnp.exp(scores - row_peak), 0.0)
        totals = jnp.sum(weights, axis=-1)
        rounded = lax.optimization_barrier(weights.astype(jnp.bfloat16))
        mixed_rows = jnp.einsum("grm,md->grd", rounded.astype(jnp.float32), value_part.astype(jnp.float32))
        safe_totals = jnp.where(totals > 0.0, totals, 1.0)
        return mixed_rows / safe_totals[..., None]

    results = lax.map(one_block, jnp.arange(KVH * block_count, dtype=jnp.int32))
    results = results.reshape(KVH, block_count, group_size, block_rows, HD)
    return jnp.transpose(results, (1, 3, 0, 2, 4)).reshape(total_rows, KVH * group_size * HD)


def reference(query_self, key_self, value_self, positions, query_cross, key_vision, value_vision, media_range, gate_scale):
    group_size = HQ // KVH
    rotated_query = rotate(query_self.astype(jnp.float32).reshape(TEXT, HQ, HD), positions)
    rotated_query = rotated_query.astype(jnp.bfloat16).reshape(TEXT, KVH, group_size, HD)
    rotated_key = rotate(key_self.astype(jnp.float32).reshape(TEXT, KVH, HD), positions).astype(jnp.bfloat16)
    text_index = jnp.arange(TEXT, dtype=jnp.int32)

    def causal_rows(row_begin, block_rows):
        row_index = row_begin + jnp.arange(block_rows, dtype=jnp.int32)
        return text_index[None, :] <= row_index[:, None]

    self_context = blocked(rotated_query, rotated_key, value_self.reshape(TEXT, KVH, HD), causal_rows).astype(jnp.bfloat16)
    lower_frame = jnp.repeat(media_range[:, 0], TBLOCK)
    upper_frame = jnp.repeat(media_range[:, 1], TBLOCK)
    frame_index = jnp.arange(VIS, dtype=jnp.int32) // FRAME_LEN

    def frame_rows(row_begin, block_rows):
        lower_part = lax.dynamic_slice_in_dim(lower_frame, row_begin, block_rows, 0)
        upper_part = lax.dynamic_slice_in_dim(upper_frame, row_begin, block_rows, 0)
        return jnp.logical_and(frame_index[None, :] >= lower_part[:, None], frame_index[None, :] < upper_part[:, None])

    cross = blocked(query_cross.reshape(TEXT, KVH, group_size, HD), key_vision.reshape(VIS, KVH, HD), value_vision.reshape(VIS, KVH, HD), frame_rows)
    has_frames = upper_frame > lower_frame
    cross_context = jnp.where(has_frames[:, None], jnp.tanh(gate_scale[0]) * cross, 0.0).astype(jnp.bfloat16)
    return self_context, cross_context
```

```python
import functools
import math

import jax
import jax.numpy as jnp
from jax import lax
from jax.experimental import pallas as pl
from jax.experimental.pallas import tpu as pltpu
from jax.sharding import PartitionSpec as P

HD = 128
TBLOCK = 16
FRAME_LEN = 896
NY = 4
ROPE_BASE = 500000.0
BIG = 1e30
LOWEST = -3e38
LOG2 = HD ** -0.5 * math.log2(math.e)
MESH = pl.DeviceIdType.MESH
F32 = jnp.float32
BF16 = jnp.bfloat16


def prepare_kernel(qs, ks, vs, qc, kf, vf, cos, sin, qa, o_qs, o_qc, o_kv):
    rows = qs.shape[0]
    heads = qs.shape[1] // HD
    cosine = cos[...]
    sine = sin[...]

    def turned(x):
        x = x.astype(F32)
        return (x * cosine + pltpu.roll(x, HD // 2, 1) * sine).astype(BF16)

    o_kv[0:rows, 0:HD] = turned(ks[...])
    o_kv[0:rows, HD:] = vs[...]
    pad = jnp.zeros((rows - kf.shape[0], HD), F32)
    o_kv[rows:, 0:HD] = jnp.concatenate([kf[...].astype(F32), pad], 0).astype(BF16)
    o_kv[rows:, HD:] = jnp.concatenate([vf[...].astype(F32), pad], 0).astype(BF16)
    for h in range(heads):
        cut = slice(h * HD, (h + 1) * HD)
        o_qs[:, cut] = turned(qs[:, cut])
    o_qc[:, 0 : heads * HD] = qc[...]
    o_qc[:, heads * HD :] = qa[...]


def main_kernel(
    nz, ny, nh, real, zpf,
    qs, qc, kv, gate, out_s, out_c,
    kvb, qsb, qcb, qat, m_s, l_s, acc_s, m_c, l_c, acc_c,
    osb, ocb, stb, rsb, rcb, rst, fsb, fcb,
    r_ring, s_ring, r_q, s_q, r_o, s_o, r_f, s_f, loc,
):
    rows = qs.shape[0]
    heads = qs.shape[1] // HD
    toks = ny * rows
    half = nz // 2
    groups = nz // 4
    ctx = lax.axis_index("ctx")
    head = lax.axis_index("head")
    z = ctx // ny
    y = ctx % ny
    z_up = (z + 1) % nz
    z_dn = (z + nz - 1) % nz

    def at_z(other):
        return (other * ny + y, head)

    def at_y(other):
        return (z * ny + other, head)

    def at_h(other):
        return (ctx, other)

    def slot(offset):
        return (z + nz + offset) % nz

    def ring(flow, d, piece):
        src_slot = slot(d - 1) if flow == 0 else slot(1 - d)
        part = pl.ds(piece * rows, rows)
        return pltpu.make_async_remote_copy(
            src_ref=kvb.at[src_slot, part, :],
            dst_ref=kvb.at[src_slot, part, :],
            send_sem=s_ring.at[flow, d, piece],
            recv_sem=r_ring.at[flow, d, piece],
            device_id=at_z(z_dn if flow == 0 else z_up),
            device_id_type=MESH,
        )

    def ring_in(flow, d, piece):
        dst_slot = slot(d) if flow == 0 else slot(-d)
        part = pl.ds(piece * rows, rows)
        return pltpu.make_async_remote_copy(
            src_ref=kvb.at[dst_slot, part, :],
            dst_ref=kvb.at[dst_slot, part, :],
            send_sem=s_ring.at[flow, d, piece],
            recv_sem=r_ring.at[flow, d, piece],
            device_id=at_z(z_dn if flow == 0 else z_up),
            device_id_type=MESH,
        )

    def q_copy(kind, i):
        src, dst = ((qs, qsb), (qc, qcb))[kind]
        return pltpu.make_async_remote_copy(
            src_ref=src,
            dst_ref=dst.at[y],
            send_sem=s_q.at[kind, i],
            recv_sem=r_q.at[kind, i],
            device_id=at_y((y + i) % ny),
            device_id_type=MESH,
        )

    def q_in(kind, i):
        src, dst = ((qs, qsb), (qc, qcb))[kind]
        return pltpu.make_async_remote_copy(
            src_ref=src,
            dst_ref=dst.at[(y + ny - i) % ny],
            send_sem=s_q.at[kind, i],
            recv_sem=r_q.at[kind, i],
            device_id=at_y((y + i) % ny),
            device_id_type=MESH,
        )

    def o_copy(kind, i):
        src, dst = ((osb, rsb), (ocb, rcb), (stb, rst))[kind]
        return pltpu.make_async_remote_copy(
            src_ref=src.at[(y + i) % ny],
            dst_ref=dst.at[i],
            send_sem=s_o.at[kind, i],
            recv_sem=r_o.at[kind, i],
            device_id=at_y((y + i) % ny),
            device_id_type=MESH,
        )

    wide = heads * HD

    def f_copy(kind, i):
        src, dst = ((fsb, out_s), (fcb, out_c))[kind]
        other = (head + i) % nh
        return pltpu.make_async_remote_copy(
            src_ref=src.at[other],
            dst_ref=dst.at[:, pl.ds(pl.multiple_of(head * wide, wide), wide)],
            send_sem=s_f.at[kind, i],
            recv_sem=r_f.at[kind, i],
            device_id=at_h(other),
            device_id_type=MESH,
        )

    def f_in(kind, i):
        src, dst = ((fsb, out_s), (fcb, out_c))[kind]
        other = (head + nh - i) % nh
        return pltpu.make_async_remote_copy(
            src_ref=src.at[other],
            dst_ref=dst.at[:, pl.ds(pl.multiple_of(other * wide, wide), wide)],
            send_sem=s_f.at[kind, i],
            recv_sem=r_f.at[kind, i],
            device_id=at_h((head + i) % nh),
            device_id_type=MESH,
        )

    own_kv = pltpu.make_async_copy(kv, kvb.at[z], loc.at[0])
    own_qs = pltpu.make_async_copy(qs, qsb.at[y], loc.at[1])
    own_qc = pltpu.make_async_copy(qc, qcb.at[y], loc.at[2])
    own_kv.start()
    own_qs.start()
    own_qc.start()

    barrier = pltpu.get_barrier_semaphore()
    partners = [at_z(z_up), at_z(z_dn)]
    partners += [at_y((y + i) % ny) for i in range(1, ny)]
    partners += [at_h((head + i) % nh) for i in range(1, nh)]
    for partner in partners:
        pl.semaphore_signal(barrier, inc=1, device_id=partner, device_id_type=MESH)
    pl.semaphore_wait(barrier, len(partners))

    own_kv.wait()
    for piece in range(2):
        ring(0, 1, piece).start()
        ring(1, 1, piece).start()
    for kind in range(2):
        for i in range(1, ny):
            q_copy(kind, i).start()

    lane = lax.broadcasted_iota(jnp.int32, (toks, HD), 1)
    token = lax.broadcasted_iota(jnp.int32, (toks, HD), 0)
    late = jnp.logical_and(lane < nz, lane > z)
    ahead = jnp.logical_and(lane >= rows, y * rows + lane - rows > token)
    qat[...] = jnp.where(jnp.logical_or(late, ahead), -BIG, 0.0).astype(BF16)

    @pl.loop(0, heads)
    def _(h):
        m_s[h] = jnp.full((toks, HD), LOWEST, F32)
        m_c[h] = jnp.full((toks, HD), LOWEST, F32)
        l_s[h] = jnp.zeros((toks, HD), F32)
        l_c[h] = jnp.zeros((toks, HD), F32)
        acc_s[h] = jnp.zeros((toks, HD), F32)
        acc_c[h] = jnp.zeros((toks, HD), F32)

    own_qs.wait()
    own_qc.wait()

    def serve(d, piece):
        ring_in(0, d, piece).wait_recv()

        @pl.when(d < half)
        def _():
            ring(0, d + 1, piece).start()

        @pl.when(d < half)
        def _():
            ring_in(1, d, piece).wait_recv()

        @pl.when(d < half - 1)
        def _():
            ring(1, d + 1, piece).start()

    def keys_of(kind, group):
        offsets = (-2 * group, -2 * group - 1, 2 * group + 1, 2 * group + 2)
        keys, marks, values = [], [], []
        lanes = lax.broadcasted_iota(jnp.int32, (rows, HD), 1)
        index = lax.broadcasted_iota(jnp.int32, (rows, HD), 0)
        for offset in offsets:
            at = slot(offset)
            part = slice(kind * rows, (kind + 1) * rows)
            keys.append(kvb[at, part, 0:HD])
            values.append(kvb[at, part, HD:])
            if kind == 0:
                mark = jnp.where(at == z, rows + index, at)
            else:
                mark = jnp.where(index < real, at // zpf, HD - 1)
            marks.append(jnp.where(lanes == mark, 1.0, 0.0).astype(BF16))
        key = jnp.concatenate([jnp.concatenate(keys, 0), jnp.concatenate(marks, 0)], 1)
        return key, jnp.concatenate(values, 0)

    def attend(kind, group, head_list):
        key, value = keys_of(kind, group)
        qb = (qsb, qcb)[kind]
        m_r, l_r, acc_r = ((m_s, l_s, acc_s), (m_c, l_c, acc_c))[kind]
        if kind == 0:
            extra = qat[...]
        else:
            extra = qcb[:, :, wide:].reshape(toks, HD)
        for h in head_list:
            q = qb[:, :, h * HD : (h + 1) * HD].reshape(toks, HD)
            scores = lax.dot_general(
                jnp.concatenate([q, extra], 1), key,
                (((1,), (1,)), ((), ())), preferred_element_type=F32,
            )
            m_old = m_r[h]
            m_new = jnp.maximum(m_old, jnp.max(scores, axis=1, keepdims=True))
            m_r[h] = m_new
            alpha = jnp.exp2((m_old - m_new) * LOG2)
            weights = jnp.exp2((scores - m_new[:, 0:1]) * LOG2)
            total = weights[:, 0:HD]
            for b in range(1, weights.shape[1] // HD):
                total = total + weights[:, b * HD : (b + 1) * HD]
            l_r[h] = l_r[h] * alpha + total
            acc_r[h] = acc_r[h] * alpha + jnp.dot(
                weights.astype(BF16), value, preferred_element_type=F32
            )

    low = tuple(range(heads // 2))
    high = tuple(range(heads // 2, heads))

    @pl.loop(0, groups + 1)
    def _(g):
        for turn in range(4):
            @pl.when(g < groups)
            def _():
                serve(2 * g + 1 + turn // 2, turn % 2)

            if turn % 2 == 0:
                @pl.when(g == 1)
                def _():
                    for i in range(1, ny):
                        q_in(turn // 2, i).wait_recv()

            @pl.when(g > 0)
            def _():
                attend(turn // 2, g - 1, (low, high)[turn % 2])

    lane = lax.broadcasted_iota(jnp.int32, (toks, HD), 1)
    stats = jnp.zeros((toks, HD), F32)
    for kind in range(2):
        m_r, l_r, acc_r = ((m_s, l_s, acc_s), (m_c, l_c, acc_c))[kind]
        dst = (osb, ocb)[kind]
        for h in range(heads):
            total = jnp.sum(l_r[h], axis=1, keepdims=True)
            part = acc_r[h] / total
            dst[:, :, h * HD : (h + 1) * HD] = part.astype(BF16).reshape(ny, rows, HD)
            level = m_r[h] * LOG2 + jnp.log2(total)
            stats = jnp.where(lane == kind * heads + h, level, stats)
        if kind == 1:
            stb[...] = stats.reshape(ny, rows, HD)
        for i in range(1, ny):
            o_copy(kind, i).start()
    for i in range(1, ny):
        o_copy(2, i).start()

    for i in range(1, ny):
        o_copy(2, i).wait_recv()
    levels = [stb[y]] + [rst[i] for i in range(1, ny)]
    top = levels[0]
    for level in levels[1:]:
        top = jnp.maximum(top, level)
    shares = [jnp.exp2(level - top) for level in levels]
    whole = shares[0]
    for share in shares[1:]:
        whole = whole + share
    shares = [share / whole for share in shares]
    for kind in range(2):
        mine, other = ((osb, rsb), (ocb, rcb))[kind]
        final, out = ((fsb, out_s), (fcb, out_c))[kind]
        for i in range(1, ny):
            o_copy(kind, i).wait_recv()
        for h in range(heads):
            cut = slice(h * HD, (h + 1) * HD)
            at = kind * heads + h
            mixed = mine[y, :, cut].astype(F32) * shares[0][:, at : at + 1]
            for i in range(1, ny):
                mixed = mixed + other[i, :, cut].astype(F32) * shares[i][:, at : at + 1]
            if kind == 1:
                mixed = mixed * gate[...]
            final[:, :, cut] = mixed.reshape(nh, rows // nh, HD).astype(BF16)
        for i in range(1, nh):
            f_copy(kind, i).start()
        pltpu.make_async_copy(
            final.at[head],
            out.at[:, pl.ds(pl.multiple_of(head * wide, wide), wide)],
            loc.at[3 + kind],
        ).start()
    for kind in range(2):
        final, out = ((fsb, out_s), (fcb, out_c))[kind]
        for i in range(1, nh):
            f_in(kind, i).wait_recv()
        pltpu.make_async_copy(
            final.at[head],
            out.at[:, pl.ds(pl.multiple_of(head * wide, wide), wide)],
            loc.at[3 + kind],
        ).wait()

    @pl.loop(1, half)
    def _(d):
        for flow in range(2):
            for piece in range(2):
                ring(flow, d, piece).wait_send()

    for piece in range(2):
        ring(0, half, piece).wait_send()
    for kind in range(2):
        for i in range(1, ny):
            q_copy(kind, i).wait_send()
    for kind in range(3):
        for i in range(1, ny):
            o_copy(kind, i).wait_send()
    for kind in range(2):
        for i in range(1, nh):
            f_copy(kind, i).wait_send()


def on_device(
    nctx, nh,
    query_self, key_self, value_self, positions,
    query_cross, key_vision, value_vision, media_range, gate_scale,
):
    rows, wide = query_self.shape
    real = key_vision.shape[0]
    ny = NY
    nz = nctx // ny
    heads = wide // HD
    toks = ny * rows
    zpf = FRAME_LEN // (real * ny)

    exponents = jnp.arange(HD // 2, dtype=F32) * (2.0 / HD)
    frequency = jnp.power(ROPE_BASE, -exponents)
    angles = positions.astype(F32)[:, None] * jnp.tile(frequency, 2)[None, :]
    first = jnp.arange(HD)[None, :] < HD // 2
    cosine = jnp.cos(angles)
    sine = jnp.where(first, -jnp.sin(angles), jnp.sin(angles))

    lower = jnp.repeat(media_range[:, 0], TBLOCK)[:, None]
    upper = jnp.repeat(media_range[:, 1], TBLOCK)[:, None]
    lanes = jnp.arange(HD, dtype=jnp.int32)[None, :]
    hidden = jnp.logical_or(lanes < lower, lanes >= upper)
    hidden = jnp.logical_and(hidden, lanes < nz // zpf)
    hidden = jnp.logical_or(hidden, lanes == HD - 1)
    extra = jnp.where(hidden, -BIG, 0.0).astype(BF16)
    gate = jnp.where(upper > lower, jnp.tanh(gate_scale[0]), 0.0)
    gate = jnp.broadcast_to(gate, (rows, HD)).astype(F32)

    vmem = pl.BlockSpec(memory_space=pltpu.VMEM)
    qs, qc, kv = pl.pallas_call(
        prepare_kernel,
        out_shape=(
            jax.ShapeDtypeStruct((rows, wide), BF16),
            jax.ShapeDtypeStruct((rows, wide + HD), BF16),
            jax.ShapeDtypeStruct((2 * rows, 2 * HD), BF16),
        ),
        in_specs=[vmem] * 9,
        out_specs=(vmem,) * 3,
        name="prepare",
    )(query_self, key_self, value_self, query_cross, key_vision, value_vision, cosine, sine, extra)

    state = pltpu.VMEM((heads, toks, HD), F32)
    part = pltpu.VMEM((ny, rows, wide), BF16)
    stat = pltpu.VMEM((ny, rows, HD), F32)
    final = pltpu.VMEM((nh, rows // nh, wide), BF16)
    dma = pltpu.SemaphoreType.DMA
    half = nz // 2
    return pl.pallas_call(
        functools.partial(main_kernel, nz, ny, nh, real, zpf),
        out_shape=(jax.ShapeDtypeStruct((rows // nh, wide * nh), BF16),) * 2,
        in_specs=[vmem] * 4,
        out_specs=(vmem,) * 2,
        scratch_shapes=[
            pltpu.VMEM((nz, 2 * rows, 2 * HD), BF16),
            part,
            pltpu.VMEM((ny, rows, wide + HD), BF16),
            pltpu.VMEM((toks, HD), BF16),
            state, state, state, state, state, state,
            part, part, stat, part, part, stat, final, final,
            dma((2, half + 1, 2)), dma((2, half + 1, 2)),
            dma((2, ny)), dma((2, ny)),
            dma((3, ny)), dma((3, ny)),
            dma((2, nh)), dma((2, nh)),
            dma((5,)),
        ],
        compiler_params=pltpu.CompilerParams(
            collective_id=0, has_side_effects=True, vmem_limit_bytes=40 * 1024 * 1024
        ),
        name="attend",
    )(qs, qc, kv, gate)


def solution(mesh):
    placed = (
        P("ctx", "head"),
        P("ctx", "head"),
        P("ctx", "head"),
        P("ctx"),
        P("ctx", "head"),
        P("ctx", "head"),
        P("ctx", "head"),
        P("ctx", None),
        P(),
    )
    body = functools.partial(on_device, mesh.shape["ctx"], mesh.shape["head"])
    return jax.shard_map(
        body,
        mesh=mesh,
        in_specs=placed,
        out_specs=(P(("ctx", "head"), None), P(("ctx", "head"), None)),
        check_vma=False,
    )
```

```python
import functools
import math

import jax
import jax.numpy as jnp
from jax import lax
from jax.experimental import pallas as pl
from jax.experimental.pallas import tpu as pltpu
from jax.sharding import PartitionSpec as P

HD = 128
TBLOCK = 16
FRAME_LEN = 896
NY = 4
ROPE_BASE = 500000.0
BIG = 1e30
LOWEST = -3e38
LOG2 = HD ** -0.5 * math.log2(math.e)
MESH = pl.DeviceIdType.MESH
F32 = jnp.float32
BF16 = jnp.bfloat16


def prepare_kernel(qs, ks, vs, qc, kf, vf, cos, sin, qa, o_qs, o_qc, o_kv):
    rows = qs.shape[0]
    heads = qs.shape[1] // HD
    cosine = cos[...]
    sine = sin[...]

    def turned(x):
        x = x.astype(F32)
        return (x * cosine + pltpu.roll(x, HD // 2, 1) * sine).astype(BF16)

    o_kv[0:rows, 0:HD] = turned(ks[...])
    o_kv[0:rows, HD:] = vs[...]
    pad = jnp.zeros((rows - kf.shape[0], HD), F32)
    o_kv[rows:, 0:HD] = jnp.concatenate([kf[...].astype(F32), pad], 0).astype(BF16)
    o_kv[rows:, HD:] = jnp.concatenate([vf[...].astype(F32), pad], 0).astype(BF16)
    for h in range(heads):
        cut = slice(h * HD, (h + 1) * HD)
        o_qs[:, cut] = turned(qs[:, cut])
    o_qc[:, 0 : heads * HD] = qc[...]
    o_qc[:, heads * HD :] = qa[...]


def main_kernel(
    nz, ny, nh, real, zpf,
    qs, qc, kv, gate, out_s, out_c,
    kvb, qsb, qcb, qat, m_s, l_s, acc_s, m_c, l_c, acc_c,
    scb, rel, osb, ocb, stb, rsb, rcb, rst, fsb, fcb,
    r_ring, s_ring, r_q, s_q, r_o, s_o, r_r, s_r, r_f, s_f, loc,
):
    rows = qs.shape[0]
    wide = qs.shape[1]
    heads = wide // HD
    packed = heads // 2
    span = packed * rows
    half = nz // 2
    groups = nz // 4
    ctx = lax.axis_index("ctx")
    head = lax.axis_index("head")
    z = ctx // ny
    y = ctx % ny
    z_up = (z + 1) % nz
    z_dn = (z + nz - 1) % nz

    def at_z(other):
        return (other * ny + y, head)

    def at_y(i):
        return (z * ny + (y + i) % ny, head)

    def at_h(i):
        return (ctx, (head + i) % nh)

    def slot(offset):
        return (z + nz + offset) % nz

    def ring(flow, d, piece, first=False):
        at = slot(d - 1) if flow == 0 else slot(1 - d)
        part = pl.ds(piece * rows, rows)
        return pltpu.make_async_remote_copy(
            src_ref=kv.at[part, :] if first else kvb.at[at, part, :],
            dst_ref=kvb.at[at, part, :],
            send_sem=s_ring.at[flow, d, piece],
            recv_sem=r_ring.at[flow, d, piece],
            device_id=at_z(z_dn if flow == 0 else z_up),
            device_id_type=MESH,
        )

    def ring_in(flow, d, piece):
        at = slot(d) if flow == 0 else slot(-d)
        part = pl.ds(piece * rows, rows)
        return pltpu.make_async_remote_copy(
            src_ref=kvb.at[at, part, :],
            dst_ref=kvb.at[at, part, :],
            send_sem=s_ring.at[flow, d, piece],
            recv_sem=r_ring.at[flow, d, piece],
            device_id=at_z(z_dn if flow == 0 else z_up),
            device_id_type=MESH,
        )

    def q_copy(kind, i):
        src, dst = ((qs, qsb), (qc, qcb))[kind]
        return pltpu.make_async_remote_copy(
            src_ref=src,
            dst_ref=dst.at[ny - i],
            send_sem=s_q.at[kind, ny - i],
            recv_sem=r_q.at[kind, ny - i],
            device_id=at_y(i),
            device_id_type=MESH,
        )

    def q_relay(kind):
        dst = (qsb, qcb)[kind]
        came, goes = ((ny - 1, 1), (1, ny - 1))[kind]
        return pltpu.make_async_remote_copy(
            src_ref=dst.at[came],
            dst_ref=dst.at[2],
            send_sem=s_q.at[kind, 2],
            recv_sem=r_q.at[kind, 2],
            device_id=at_y(goes),
            device_id_type=MESH,
        )

    def o_copy(kind, i):
        src, dst = ((osb, rsb), (ocb, rcb))[kind]
        return pltpu.make_async_remote_copy(
            src_ref=src.at[i],
            dst_ref=dst.at[ny - i],
            send_sem=s_o.at[kind, ny - i],
            recv_sem=r_o.at[kind, ny - i],
            device_id=at_y(i),
            device_id_type=MESH,
        )

    def o_half(kind, j):
        src = (osb, ocb)[kind]
        return pltpu.make_async_remote_copy(
            src_ref=src.at[2, :, pl.ds(j * span, span)],
            dst_ref=rel.at[kind, j],
            send_sem=s_r.at[kind, j],
            recv_sem=r_r.at[kind, j],
            device_id=at_y((1, ny - 1)[j]),
            device_id_type=MESH,
        )

    def o_relay(kind, j):
        dst = (rsb, rcb)[kind]
        return pltpu.make_async_remote_copy(
            src_ref=rel.at[kind, j],
            dst_ref=dst.at[2, :, pl.ds(j * span, span)],
            send_sem=s_r.at[kind, 2 + j],
            recv_sem=r_r.at[kind, 2 + j],
            device_id=at_y((1, ny - 1)[j]),
            device_id_type=MESH,
        )

    def t_copy(kind, i):
        return pltpu.make_async_remote_copy(
            src_ref=stb.at[kind, i],
            dst_ref=rst.at[kind, ny - i],
            send_sem=s_o.at[2 + kind, ny - i],
            recv_sem=r_o.at[2 + kind, ny - i],
            device_id=at_y(i),
            device_id_type=MESH,
        )

    def f_copy(kind, i):
        src, dst = ((fsb, out_s), (fcb, out_c))[kind]
        return pltpu.make_async_remote_copy(
            src_ref=src.at[(head + i) % nh],
            dst_ref=dst.at[:, pl.ds(pl.multiple_of(head * wide, wide), wide)],
            send_sem=s_f.at[kind, i],
            recv_sem=r_f.at[kind, i],
            device_id=at_h(i),
            device_id_type=MESH,
        )

    def f_in(kind, i):
        src, dst = ((fsb, out_s), (fcb, out_c))[kind]
        other = (head + nh - i) % nh
        return pltpu.make_async_remote_copy(
            src_ref=src.at[other],
            dst_ref=dst.at[:, pl.ds(pl.multiple_of(other * wide, wide), wide)],
            send_sem=s_f.at[kind, i],
            recv_sem=r_f.at[kind, i],
            device_id=at_h(i),
            device_id_type=MESH,
        )

    own_kv = pltpu.make_async_copy(kv, kvb.at[z], loc.at[0])
    own_qs = pltpu.make_async_copy(qs, qsb.at[0], loc.at[1])
    own_qc = pltpu.make_async_copy(qc, qcb.at[0], loc.at[2])
    own_kv.start()
    own_qs.start()
    own_qc.start()

    barrier = pltpu.get_barrier_semaphore()
    partners = [at_z(z_up), at_z(z_dn)]
    partners += [at_y(i) for i in range(1, ny)]
    partners += [at_h(i) for i in range(1, nh)]
    for partner in partners:
        pl.semaphore_signal(barrier, inc=1, device_id=partner, device_id_type=MESH)
    pl.semaphore_wait(barrier, len(partners))

    for piece in range(2):
        ring(0, 1, piece, True).start()
        ring(1, 1, piece, True).start()
    for kind in range(2):
        for i in (1, ny - 1):
            q_copy(kind, i).start()

    lane = lax.broadcasted_iota(jnp.int32, (rows, HD), 1)
    token = lax.broadcasted_iota(jnp.int32, (rows, HD), 0)
    late = jnp.logical_and(lane < nz, lane > z)
    for i in range(ny):
        place = ((y + i) % ny - y) * rows + token
        ahead = jnp.logical_and(lane >= rows, lane - rows > place)
        qat[i] = jnp.where(jnp.logical_or(late, ahead), -BIG, 0.0).astype(BF16)
    for m_r, l_r in ((m_s, l_s), (m_c, l_c)):
        m_r[...] = jnp.full(m_r.shape, LOWEST, F32)
        l_r[...] = jnp.zeros(l_r.shape, F32)

    @pl.loop(0, 2 * ny)
    def _(b):
        acc_s[b] = jnp.zeros((HD, span), F32)
        acc_c[b] = jnp.zeros((HD, span), F32)

    own_kv.wait()
    own_qs.wait()
    own_qc.wait()

    def serve(d, piece):
        ring_in(0, d, piece).wait_recv()

        @pl.when(d < half)
        def _():
            ring(0, d + 1, piece).start()

        @pl.when(d < half)
        def _():
            ring_in(1, d, piece).wait_recv()

        @pl.when(d < half - 1)
        def _():
            ring(1, d + 1, piece).start()

    def keys_of(kind, group):
        offsets = (-2 * group, -2 * group - 1, 2 * group + 1, 2 * group + 2)
        keys, marks, values = [], [], []
        lanes = lax.broadcasted_iota(jnp.int32, (rows, HD), 1)
        index = lax.broadcasted_iota(jnp.int32, (rows, HD), 0)
        for offset in offsets:
            at = slot(offset)
            part = slice(kind * rows, (kind + 1) * rows)
            keys.append(kvb[at, part, 0:HD])
            values.append(kvb[at, part, HD:])
            if kind == 0:
                mark = jnp.where(at == z, rows + index, at)
            else:
                mark = jnp.where(index < real, at // zpf, HD - 1)
            marks.append(jnp.where(lanes == mark, 1.0, 0.0).astype(BF16))
        key = jnp.concatenate([jnp.concatenate(keys, 0), jnp.concatenate(marks, 0)], 1)
        value = jnp.concatenate(values, 0).astype(F32)
        return key, jnp.transpose(value).astype(BF16)

    def q_wait(kind, i):
        if i == 2:
            q_relay(kind).wait_recv()
        elif i > 0:
            q_copy(kind, ny - i).wait_recv()

    def attend(kind, group, sources):
        key, value = keys_of(kind, group)
        qb = (qsb, qcb)[kind]
        m_r, l_r, acc_r = ((m_s, l_s, acc_s), (m_c, l_c, acc_c))[kind]

        def score(i, j, turn):
            b = 2 * i + j
            extra = qat[i] if kind == 0 else qcb[i, :, wide:]
            parts = [
                qb[i, :, h * HD : (h + 1) * HD]
                for h in range(j * packed, (j + 1) * packed)
            ]
            q = jnp.concatenate(
                [jnp.concatenate(parts, 0), jnp.concatenate([extra] * packed, 0)], 1
            )
            scores = lax.dot_general(
                key, q, (((1,), (1,)), ((), ())), preferred_element_type=F32
            )
            scb[turn] = scores
            m_old = m_r[b : b + 1, :]
            m_new = jnp.maximum(m_old, jnp.max(scores, axis=0, keepdims=True))
            m_r[b : b + 1, :] = m_new
            return m_new, jnp.exp2((m_old - m_new) * LOG2)

        def fold(i, j, turn, m_new, alpha):
            b = 2 * i + j
            weights = jnp.exp2((scb[turn] - m_new) * LOG2)
            l_r[b : b + 1, :] = l_r[b : b + 1, :] * alpha + jnp.sum(
                weights, axis=0, keepdims=True
            )
            acc_r[b] = acc_r[b] * alpha + jnp.dot(
                value, weights.astype(BF16), preferred_element_type=F32
            )

        blocks = [(i, j) for i in sources for j in range(2)]
        held = score(*blocks[0], 0)
        for n, block in enumerate(blocks):
            coming = None
            if n + 1 < len(blocks):
                coming = score(*blocks[n + 1], (n + 1) % 2)
            fold(*block, n % 2, *held)
            held = coming

    def send_off(kind):
        m_r, l_r, acc_r = ((m_s, l_s, acc_s), (m_c, l_c, acc_c))[kind]
        dst = (osb, ocb)[kind]
        for i in (2, 1, ny - 1, 0):
            for j in range(2):
                b = 2 * i + j
                cut = slice(j * span, (j + 1) * span)
                total = l_r[b : b + 1, :]
                dst[i, :, cut] = (acc_r[b] / total).astype(BF16)
                stb[kind, i, :, cut] = m_r[b : b + 1, :] * LOG2 + jnp.log2(total)
        for j in range(2):
            o_half(kind, j).start()
        for i in range(1, ny):
            t_copy(kind, i).start()
        for i in (1, ny - 1):
            o_copy(kind, i).start()

    def pass_on(kind):
        for j in range(2):
            o_half(kind, j).wait_recv()
            o_relay(kind, j).start()

    low = (0, 1)
    high = (ny - 1, 2)

    @pl.loop(0, groups)
    def _(g):
        for turn in range(4):
            serve(2 * g + 1 + turn // 2, turn % 2)
            kind = turn // 2
            sources = (low, high)[turn % 2]
            if turn == 3:
                @pl.when(g == 0)
                def _():
                    q_wait(0, ny - 1)
                    q_relay(0).start()

            if turn == 1:
                @pl.when(g == 1)
                def _():
                    q_wait(1, 1)
                    q_relay(1).start()

            @pl.when(g == kind + 1)
            def _():
                for i in sources:
                    if i != (ny - 1, 1)[kind]:
                        q_wait(kind, i)

            @pl.when(g > kind)
            def _():
                attend(kind, g - 1 - kind, sources)

    attend(0, groups - 1, low + high)
    send_off(0)
    attend(1, groups - 2, low + high)
    pass_on(0)
    attend(1, groups - 1, low + high)
    send_off(1)

    for kind in range(2):
        mine, other = ((osb, rsb), (ocb, rcb))[kind]
        final, out = ((fsb, out_s), (fcb, out_c))[kind]
        for i in range(1, ny):
            t_copy(kind, ny - i).wait_recv()
        levels = [stb[kind, 0]] + [rst[kind, i] for i in range(1, ny)]
        top = levels[0]
        for level in levels[1:]:
            top = jnp.maximum(top, level)
        shares = [jnp.exp2(level - top) for level in levels]
        whole = shares[0]
        for share in shares[1:]:
            whole = whole + share
        shares = [share / whole for share in shares]
        for i in (1, ny - 1):
            o_copy(kind, ny - i).wait_recv()
        for j in range(2):
            o_relay(kind, j).wait_recv()
        for pair in range(heads // 2):
            cut = slice(pair * 2 * rows, (pair + 1) * 2 * rows)
            mixed = mine[0, :, cut].astype(F32) * shares[0][:, cut]
            for i in range(1, ny):
                mixed = mixed + other[i, :, cut].astype(F32) * shares[i][:, cut]
            mixed = jnp.transpose(mixed)
            for k in range(2):
                h = 2 * pair + k
                block = mixed[k * rows : (k + 1) * rows, :]
                if kind == 1:
                    block = block * gate[...]
                final[:, :, h * HD : (h + 1) * HD] = block.reshape(
                    nh, rows // nh, HD
                ).astype(BF16)
        for i in range(1, nh):
            f_copy(kind, i).start()
        if kind == 0:
            pass_on(1)
        pltpu.make_async_copy(
            final.at[head],
            out.at[:, pl.ds(pl.multiple_of(head * wide, wide), wide)],
            loc.at[3 + kind],
        ).start()
    for kind in range(2):
        final, out = ((fsb, out_s), (fcb, out_c))[kind]
        for i in range(1, nh):
            f_in(kind, i).wait_recv()
        pltpu.make_async_copy(
            final.at[head],
            out.at[:, pl.ds(pl.multiple_of(head * wide, wide), wide)],
            loc.at[3 + kind],
        ).wait()

    for piece in range(2):
        ring(0, 1, piece, True).wait_send()
        ring(1, 1, piece, True).wait_send()
        ring(0, half, piece).wait_send()

    @pl.loop(2, half)
    def _(d):
        for flow in range(2):
            for piece in range(2):
                ring(flow, d, piece).wait_send()

    for kind in range(2):
        for i in (1, ny - 1):
            q_copy(kind, i).wait_send()
            o_copy(kind, i).wait_send()
        q_relay(kind).wait_send()
        for i in range(1, ny):
            t_copy(kind, i).wait_send()
        for j in range(2):
            o_half(kind, j).wait_send()
            o_relay(kind, j).wait_send()
    for kind in range(2):
        for i in range(1, nh):
            f_copy(kind, i).wait_send()


def on_device(
    nctx, nh,
    query_self, key_self, value_self, positions,
    query_cross, key_vision, value_vision, media_range, gate_scale,
):
    rows, wide = query_self.shape
    real = key_vision.shape[0]
    ny = NY
    nz = nctx // ny
    heads = wide // HD
    zpf = FRAME_LEN // (real * ny)

    exponents = jnp.arange(HD // 2, dtype=F32) * (2.0 / HD)
    frequency = jnp.power(ROPE_BASE, -exponents)
    angles = positions.astype(F32)[:, None] * jnp.tile(frequency, 2)[None, :]
    first = jnp.arange(HD)[None, :] < HD // 2
    cosine = jnp.cos(angles)
    sine = jnp.where(first, -jnp.sin(angles), jnp.sin(angles))

    lower = jnp.repeat(media_range[:, 0], TBLOCK)[:, None]
    upper = jnp.repeat(media_range[:, 1], TBLOCK)[:, None]
    lanes = jnp.arange(HD, dtype=jnp.int32)[None, :]
    hidden = jnp.logical_or(lanes < lower, lanes >= upper)
    hidden = jnp.logical_and(hidden, lanes < nz // zpf)
    hidden = jnp.logical_or(hidden, lanes == HD - 1)
    extra = jnp.where(hidden, -BIG, 0.0).astype(BF16)
    gate = jnp.where(upper > lower, jnp.tanh(gate_scale[0]), 0.0)
    gate = jnp.broadcast_to(gate, (rows, HD)).astype(F32)

    vmem = pl.BlockSpec(memory_space=pltpu.VMEM)
    anywhere = pl.BlockSpec(memory_space=pl.ANY)
    qs, qc, kv = pl.pallas_call(
        prepare_kernel,
        out_shape=(
            jax.ShapeDtypeStruct((rows, wide), BF16),
            jax.ShapeDtypeStruct((rows, wide + HD), BF16),
            jax.ShapeDtypeStruct((2 * rows, 2 * HD), BF16),
        ),
        grid=(1,),
        in_specs=[vmem] * 9,
        out_specs=(
            pl.BlockSpec((rows, wide), lambda g: (0, 0)),
            pl.BlockSpec((rows, wide + HD), lambda g: (0, 0)),
            pl.BlockSpec((2 * rows, 2 * HD), lambda g: (0, 0)),
        ),
        name="prepare",
    )(query_self, key_self, value_self, query_cross, key_vision, value_vision, cosine, sine, extra)

    span = heads // 2 * rows
    row = pltpu.VMEM((2 * ny, span), F32)
    state = pltpu.VMEM((2 * ny, HD, span), F32)
    part = pltpu.VMEM((ny, HD, heads * rows), BF16)
    stat = pltpu.VMEM((2, ny, 1, heads * rows), F32)
    final = pltpu.VMEM((nh, rows // nh, wide), BF16)
    dma = pltpu.SemaphoreType.DMA
    half = nz // 2
    return pl.pallas_call(
        functools.partial(main_kernel, nz, ny, nh, real, zpf),
        out_shape=(jax.ShapeDtypeStruct((rows // nh, wide * nh), BF16),) * 2,
        in_specs=[anywhere] * 3 + [vmem],
        out_specs=(vmem,) * 2,
        scratch_shapes=[
            pltpu.VMEM((nz, 2 * rows, 2 * HD), BF16),
            pltpu.VMEM((ny, rows, wide), BF16),
            pltpu.VMEM((ny, rows, wide + HD), BF16),
            pltpu.VMEM((ny, rows, HD), BF16),
            row, row, state, row, row, state,
            pltpu.VMEM((2, 4 * rows, span), F32),
            pltpu.VMEM((2, 2, HD, span), BF16),
            part, part, stat, part, part, stat, final, final,
            dma((2, half + 1, 2)), dma((2, half + 1, 2)),
            dma((2, ny)), dma((2, ny)),
            dma((4, ny)), dma((4, ny)),
            dma((2, 4)), dma((2, 4)),
            dma((2, nh)), dma((2, nh)),
            dma((5,)),
        ],
        compiler_params=pltpu.CompilerParams(collective_id=0, has_side_effects=True),
        name="attend",
    )(qs, qc, kv, gate)


def solution(mesh):
    placed = (
        P("ctx", "head"),
        P("ctx", "head"),
        P("ctx", "head"),
        P("ctx"),
        P("ctx", "head"),
        P("ctx", "head"),
        P("ctx", "head"),
        P("ctx", None),
        P(),
    )
    body = functools.partial(on_device, mesh.shape["ctx"], mesh.shape["head"])
    return jax.shard_map(
        body,
        mesh=mesh,
        in_specs=placed,
        out_specs=(P(("ctx", "head"), None), P(("ctx", "head"), None)),
        check_vma=False,
    )
```

```python
import functools
import math

import jax
import jax.numpy as jnp
from jax import lax
from jax.experimental import pallas as pl
from jax.experimental.pallas import tpu as pltpu
from jax.sharding import PartitionSpec as P

HD = 128
TBLOCK = 16
FRAME_LEN = 896
NY = 4
ROPE_BASE = 500000.0
BIG = 1e30
LOWEST = -3e38
LOG2 = HD ** -0.5 * math.log2(math.e)
MESH = pl.DeviceIdType.MESH
F32 = jnp.float32
BF16 = jnp.bfloat16


def prepare_kernel(qs, ks, vs, qc, kf, vf, cos, sin, qa, o_qs, o_qc, o_kv):
    rows = qs.shape[0]
    heads = qs.shape[1] // HD
    cosine = cos[...]
    sine = sin[...]

    def turned(x):
        x = x.astype(F32)
        return (x * cosine + pltpu.roll(x, HD // 2, 1) * sine).astype(BF16)

    o_kv[0:rows, 0:HD] = turned(ks[...])
    o_kv[0:rows, HD:] = vs[...]
    pad = jnp.zeros((rows - kf.shape[0], HD), F32)
    o_kv[rows:, 0:HD] = jnp.concatenate([kf[...].astype(F32), pad], 0).astype(BF16)
    o_kv[rows:, HD:] = jnp.concatenate([vf[...].astype(F32), pad], 0).astype(BF16)
    for h in range(heads):
        cut = slice(h * HD, (h + 1) * HD)
        o_qs[:, cut] = turned(qs[:, cut])
    o_qc[:, 0 : heads * HD] = qc[...]
    o_qc[:, heads * HD :] = qa[...]


def main_kernel(
    nz, ny, nh, real, zpf,
    qs, qc, kv, gate, out_s, out_c,
    kvb, qsb, qcb, qat, m_s, l_s, acc_s, m_c, l_c, acc_c,
    scb, rel, osb, ocb, stb, rsb, rcb, rst, fsb, fcb,
    r_ring, s_ring, r_q, s_q, r_o, s_o, r_r, s_r, r_f, s_f, loc,
):
    rows = qs.shape[0]
    wide = qs.shape[1]
    heads = wide // HD
    packed = heads // 2
    span = packed * rows
    half = nz // 2
    lag = 5
    ctx = lax.axis_index("ctx")
    head = lax.axis_index("head")
    z = ctx // ny
    y = ctx % ny
    z_up = (z + 1) % nz
    z_dn = (z + nz - 1) % nz

    def at_z(other):
        return (other * ny + y, head)

    def at_y(i):
        return (z * ny + (y + i) % ny, head)

    def at_h(i):
        return (ctx, (head + i) % nh)

    def slot(offset):
        return (z + nz + offset) % nz

    def ring(flow, d, piece, first=False):
        at = slot(d - 1) if flow == 0 else slot(1 - d)
        part = pl.ds(piece * rows, rows)
        return pltpu.make_async_remote_copy(
            src_ref=kv.at[part, :] if first else kvb.at[at, part, :],
            dst_ref=kvb.at[at, part, :],
            send_sem=s_ring.at[flow, d, piece],
            recv_sem=r_ring.at[flow, d, piece],
            device_id=at_z(z_dn if flow == 0 else z_up),
            device_id_type=MESH,
        )

    def ring_in(flow, d, piece):
        at = slot(d) if flow == 0 else slot(-d)
        part = pl.ds(piece * rows, rows)
        return pltpu.make_async_remote_copy(
            src_ref=kvb.at[at, part, :],
            dst_ref=kvb.at[at, part, :],
            send_sem=s_ring.at[flow, d, piece],
            recv_sem=r_ring.at[flow, d, piece],
            device_id=at_z(z_dn if flow == 0 else z_up),
            device_id_type=MESH,
        )

    def q_copy(kind, i):
        src, dst = ((qs, qsb), (qc, qcb))[kind]
        return pltpu.make_async_remote_copy(
            src_ref=src,
            dst_ref=dst.at[ny - i],
            send_sem=s_q.at[kind, ny - i],
            recv_sem=r_q.at[kind, ny - i],
            device_id=at_y(i),
            device_id_type=MESH,
        )

    def q_relay(kind):
        dst = (qsb, qcb)[kind]
        came, goes = ((ny - 1, 1), (1, ny - 1))[kind]
        return pltpu.make_async_remote_copy(
            src_ref=dst.at[came],
            dst_ref=dst.at[2],
            send_sem=s_q.at[kind, 2],
            recv_sem=r_q.at[kind, 2],
            device_id=at_y(goes),
            device_id_type=MESH,
        )

    def o_copy(kind, i):
        src, dst = ((osb, rsb), (ocb, rcb))[kind]
        return pltpu.make_async_remote_copy(
            src_ref=src.at[i],
            dst_ref=dst.at[ny - i],
            send_sem=s_o.at[kind, ny - i],
            recv_sem=r_o.at[kind, ny - i],
            device_id=at_y(i),
            device_id_type=MESH,
        )

    def o_half(kind, j):
        src = (osb, ocb)[kind]
        return pltpu.make_async_remote_copy(
            src_ref=src.at[2, :, pl.ds(j * span, span)],
            dst_ref=rel.at[kind, j],
            send_sem=s_r.at[kind, j],
            recv_sem=r_r.at[kind, j],
            device_id=at_y((1, ny - 1)[j]),
            device_id_type=MESH,
        )

    def o_relay(kind, j):
        dst = (rsb, rcb)[kind]
        return pltpu.make_async_remote_copy(
            src_ref=rel.at[kind, j],
            dst_ref=dst.at[2, :, pl.ds(j * span, span)],
            send_sem=s_r.at[kind, 2 + j],
            recv_sem=r_r.at[kind, 2 + j],
            device_id=at_y((1, ny - 1)[j]),
            device_id_type=MESH,
        )

    def t_copy(kind, i):
        return pltpu.make_async_remote_copy(
            src_ref=stb.at[kind, i],
            dst_ref=rst.at[kind, ny - i],
            send_sem=s_o.at[2 + kind, ny - i],
            recv_sem=r_o.at[2 + kind, ny - i],
            device_id=at_y(i),
            device_id_type=MESH,
        )

    def f_copy(kind, i):
        src, dst = ((fsb, out_s), (fcb, out_c))[kind]
        return pltpu.make_async_remote_copy(
            src_ref=src.at[(head + i) % nh],
            dst_ref=dst.at[:, pl.ds(pl.multiple_of(head * wide, wide), wide)],
            send_sem=s_f.at[kind, i],
            recv_sem=r_f.at[kind, i],
            device_id=at_h(i),
            device_id_type=MESH,
        )

    def f_in(kind, i):
        src, dst = ((fsb, out_s), (fcb, out_c))[kind]
        other = (head + nh - i) % nh
        return pltpu.make_async_remote_copy(
            src_ref=src.at[other],
            dst_ref=dst.at[:, pl.ds(pl.multiple_of(other * wide, wide), wide)],
            send_sem=s_f.at[kind, i],
            recv_sem=r_f.at[kind, i],
            device_id=at_h(i),
            device_id_type=MESH,
        )

    own_kv = pltpu.make_async_copy(kv, kvb.at[z], loc.at[0])
    own_qs = pltpu.make_async_copy(qs, qsb.at[0], loc.at[1])
    own_qc = pltpu.make_async_copy(qc, qcb.at[0], loc.at[2])
    own_kv.start()
    own_qs.start()
    own_qc.start()

    barrier = pltpu.get_barrier_semaphore()
    partners = [at_z(z_up), at_z(z_dn)]
    partners += [at_y(i) for i in range(1, ny)]
    partners += [at_h(i) for i in range(1, nh)]
    for partner in partners:
        pl.semaphore_signal(barrier, inc=1, device_id=partner, device_id_type=MESH)
    pl.semaphore_wait(barrier, len(partners))

    for piece in range(2):
        ring(0, 1, piece, True).start()
        ring(1, 1, piece, True).start()
    for kind in range(2):
        for i in (1, ny - 1):
            q_copy(kind, i).start()

    lane = lax.broadcasted_iota(jnp.int32, (rows, HD), 1)
    token = lax.broadcasted_iota(jnp.int32, (rows, HD), 0)
    late = jnp.logical_and(lane < nz, lane > z)
    for i in range(ny):
        place = ((y + i) % ny - y) * rows + token
        ahead = jnp.logical_and(lane >= rows, lane - rows > place)
        qat[i] = jnp.where(jnp.logical_or(late, ahead), -BIG, 0.0).astype(BF16)
    for m_r, l_r in ((m_s, l_s), (m_c, l_c)):
        m_r[...] = jnp.full(m_r.shape, LOWEST, F32)
        l_r[...] = jnp.zeros(l_r.shape, F32)

    @pl.loop(0, 2 * ny)
    def _(b):
        acc_s[b] = jnp.zeros((HD, span), F32)
        acc_c[b] = jnp.zeros((HD, span), F32)

    own_kv.wait()
    own_qs.wait()
    own_qc.wait()

    def serve_up(d, piece):
        ring_in(1, d, piece).wait_recv()

        @pl.when(d < half - 1)
        def _():
            ring(1, d + 1, piece).start()

    def serve(step, piece):
        @pl.when(step <= half)
        def _():
            ring_in(0, step, piece).wait_recv()

        @pl.when(step < half)
        def _():
            ring(0, step + 1, piece).start()

        @pl.when(jnp.logical_and(step <= z, step < half))
        def _():
            serve_up(step, piece)

        late_step = step - lag

        @pl.when(
            jnp.logical_and(late_step > z, jnp.logical_and(late_step >= 1, late_step < half))
        )
        def _():
            serve_up(late_step, piece)

    def keys_of(kind, group):
        upper, j = group
        offsets = [jnp.where(upper, 4 * j + 1 + r, -4 * j - r) for r in range(4)]
        keys, marks, values = [], [], []
        lanes = lax.broadcasted_iota(jnp.int32, (rows, HD), 1)
        index = lax.broadcasted_iota(jnp.int32, (rows, HD), 0)
        for offset in offsets:
            at = slot(offset)
            part = slice(kind * rows, (kind + 1) * rows)
            keys.append(kvb[at, part, 0:HD])
            values.append(kvb[at, part, HD:])
            if kind == 0:
                mark = jnp.where(at == z, rows + index, at)
            else:
                mark = jnp.where(index < real, at // zpf, HD - 1)
            marks.append(jnp.where(lanes == mark, 1.0, 0.0).astype(BF16))
        key = jnp.concatenate([jnp.concatenate(keys, 0), jnp.concatenate(marks, 0)], 1)
        value = jnp.concatenate(values, 0).astype(F32)
        return key, jnp.transpose(value).astype(BF16)

    def q_wait(kind, i):
        if i == 2:
            q_relay(kind).wait_recv()
        elif i > 0:
            q_copy(kind, ny - i).wait_recv()

    def attend(kind, group, sources):
        key, value = keys_of(kind, group)
        qb = (qsb, qcb)[kind]
        m_r, l_r, acc_r = ((m_s, l_s, acc_s), (m_c, l_c, acc_c))[kind]

        def score(i, j, turn):
            b = 2 * i + j
            extra = qat[i] if kind == 0 else qcb[i, :, wide:]
            parts = [
                qb[i, :, h * HD : (h + 1) * HD]
                for h in range(j * packed, (j + 1) * packed)
            ]
            q = jnp.concatenate(
                [jnp.concatenate(parts, 0), jnp.concatenate([extra] * packed, 0)], 1
            )
            scores = lax.dot_general(
                key, q, (((1,), (1,)), ((), ())), preferred_element_type=F32
            )
            scb[turn] = scores
            m_old = m_r[b : b + 1, :]
            m_new = jnp.maximum(m_old, jnp.max(scores, axis=0, keepdims=True))
            m_r[b : b + 1, :] = m_new
            return m_new, jnp.exp2((m_old - m_new) * LOG2)

        def fold(i, j, turn, m_new, alpha):
            b = 2 * i + j
            weights = jnp.exp2((scb[turn] - m_new) * LOG2)
            l_r[b : b + 1, :] = l_r[b : b + 1, :] * alpha + jnp.sum(
                weights, axis=0, keepdims=True
            )
            acc_r[b] = acc_r[b] * alpha + jnp.dot(
                value, weights.astype(BF16), preferred_element_type=F32
            )

        blocks = [(i, j) for i in sources for j in range(2)]
        held = score(*blocks[0], 0)
        for n, block in enumerate(blocks):
            coming = None
            if n + 1 < len(blocks):
                coming = score(*blocks[n + 1], (n + 1) % 2)
            fold(*block, n % 2, *held)
            held = coming

    def send_off(kind):
        m_r, l_r, acc_r = ((m_s, l_s, acc_s), (m_c, l_c, acc_c))[kind]
        dst = (osb, ocb)[kind]
        for i in (2, 1, ny - 1, 0):
            for j in range(2):
                b = 2 * i + j
                cut = slice(j * span, (j + 1) * span)
                total = l_r[b : b + 1, :]
                dst[i, :, cut] = (acc_r[b] / total).astype(BF16)
                stb[kind, i, :, cut] = m_r[b : b + 1, :] * LOG2 + jnp.log2(total)
        for j in range(2):
            o_half(kind, j).start()
        for i in range(1, ny):
            t_copy(kind, i).start()
        for i in (1, ny - 1):
            o_copy(kind, i).start()

    def pass_on(kind):
        for j in range(2):
            o_half(kind, j).wait_recv()
            o_relay(kind, j).start()

    low = (0, 1)
    high = (ny - 1, 2)

    @pl.loop(1, half + lag)
    def _(step):
        early = step < 9
        place = jnp.maximum(step - 9, 0) // 2
        upper = jnp.logical_or(early, place % 2 == 0)
        j = jnp.where(early, 0, jnp.where(upper, place // 2 + 1, place // 2))
        busy = jnp.logical_or(step >= 9, jnp.logical_or(step == 5, step == 6))
        for piece in range(2):
            serve(step, piece)
            sources = (low, high)[piece]
            if piece == 1:
                @pl.when(step == 2)
                def _():
                    q_wait(0, ny - 1)
                    q_relay(0).start()

                @pl.when(step == 3)
                def _():
                    q_wait(1, 1)
                    q_relay(1).start()

            for kind in range(2):
                @pl.when(step == 5 + kind)
                def _():
                    for i in sources:
                        if i != (ny - 1, 1)[kind]:
                            q_wait(kind, i)

                @pl.when(jnp.logical_and(busy, step % 2 == 1 - kind))
                def _():
                    attend(kind, (upper, j), sources)

    last_group = (False, nz // 8 - 1)
    attend(0, last_group, low + high)
    send_off(0)
    attend(1, last_group, low + high)
    pass_on(0)
    send_off(1)

    for kind in range(2):
        mine, other = ((osb, rsb), (ocb, rcb))[kind]
        final, out = ((fsb, out_s), (fcb, out_c))[kind]
        for i in range(1, ny):
            t_copy(kind, ny - i).wait_recv()
        levels = [stb[kind, 0]] + [rst[kind, i] for i in range(1, ny)]
        top = levels[0]
        for level in levels[1:]:
            top = jnp.maximum(top, level)
        shares = [jnp.exp2(level - top) for level in levels]
        whole = shares[0]
        for share in shares[1:]:
            whole = whole + share
        shares = [share / whole for share in shares]
        for i in (1, ny - 1):
            o_copy(kind, ny - i).wait_recv()
        for j in range(2):
            o_relay(kind, j).wait_recv()
        for pair in range(heads // 2):
            cut = slice(pair * 2 * rows, (pair + 1) * 2 * rows)
            mixed = mine[0, :, cut].astype(F32) * shares[0][:, cut]
            for i in range(1, ny):
                mixed = mixed + other[i, :, cut].astype(F32) * shares[i][:, cut]
            mixed = jnp.transpose(mixed)
            for k in range(2):
                h = 2 * pair + k
                block = mixed[k * rows : (k + 1) * rows, :]
                if kind == 1:
                    block = block * gate[...]
                final[:, :, h * HD : (h + 1) * HD] = block.reshape(
                    nh, rows // nh, HD
                ).astype(BF16)
        for i in range(1, nh):
            f_copy(kind, i).start()
        if kind == 0:
            pass_on(1)
        pltpu.make_async_copy(
            final.at[head],
            out.at[:, pl.ds(pl.multiple_of(head * wide, wide), wide)],
            loc.at[3 + kind],
        ).start()
    for kind in range(2):
        final, out = ((fsb, out_s), (fcb, out_c))[kind]
        for i in range(1, nh):
            f_in(kind, i).wait_recv()
        pltpu.make_async_copy(
            final.at[head],
            out.at[:, pl.ds(pl.multiple_of(head * wide, wide), wide)],
            loc.at[3 + kind],
        ).wait()

    for piece in range(2):
        ring(0, 1, piece, True).wait_send()
        ring(1, 1, piece, True).wait_send()
        ring(0, half, piece).wait_send()

    @pl.loop(2, half)
    def _(d):
        for flow in range(2):
            for piece in range(2):
                ring(flow, d, piece).wait_send()

    for kind in range(2):
        for i in (1, ny - 1):
            q_copy(kind, i).wait_send()
            o_copy(kind, i).wait_send()
        q_relay(kind).wait_send()
        for i in range(1, ny):
            t_copy(kind, i).wait_send()
        for j in range(2):
            o_half(kind, j).wait_send()
            o_relay(kind, j).wait_send()
    for kind in range(2):
        for i in range(1, nh):
            f_copy(kind, i).wait_send()


def on_device(
    nctx, nh,
    query_self, key_self, value_self, positions,
    query_cross, key_vision, value_vision, media_range, gate_scale,
):
    rows, wide = query_self.shape
    real = key_vision.shape[0]
    ny = NY
    nz = nctx // ny
    heads = wide // HD
    zpf = FRAME_LEN // (real * ny)

    exponents = jnp.arange(HD // 2, dtype=F32) * (2.0 / HD)
    frequency = jnp.power(ROPE_BASE, -exponents)
    angles = positions.astype(F32)[:, None] * jnp.tile(frequency, 2)[None, :]
    first = jnp.arange(HD)[None, :] < HD // 2
    cosine = jnp.cos(angles)
    sine = jnp.where(first, -jnp.sin(angles), jnp.sin(angles))

    lower = jnp.repeat(media_range[:, 0], TBLOCK)[:, None]
    upper = jnp.repeat(media_range[:, 1], TBLOCK)[:, None]
    lanes = jnp.arange(HD, dtype=jnp.int32)[None, :]
    hidden = jnp.logical_or(lanes < lower, lanes >= upper)
    hidden = jnp.logical_and(hidden, lanes < nz // zpf)
    hidden = jnp.logical_or(hidden, lanes == HD - 1)
    extra = jnp.where(hidden, -BIG, 0.0).astype(BF16)
    gate = jnp.where(upper > lower, jnp.tanh(gate_scale[0]), 0.0)
    gate = jnp.broadcast_to(gate, (rows, HD)).astype(F32)

    vmem = pl.BlockSpec(memory_space=pltpu.VMEM)
    anywhere = pl.BlockSpec(memory_space=pl.ANY)
    qs, qc, kv = pl.pallas_call(
        prepare_kernel,
        out_shape=(
            jax.ShapeDtypeStruct((rows, wide), BF16),
            jax.ShapeDtypeStruct((rows, wide + HD), BF16),
            jax.ShapeDtypeStruct((2 * rows, 2 * HD), BF16),
        ),
        grid=(1,),
        in_specs=[vmem] * 9,
        out_specs=(
            pl.BlockSpec((rows, wide), lambda g: (0, 0)),
            pl.BlockSpec((rows, wide + HD), lambda g: (0, 0)),
            pl.BlockSpec((2 * rows, 2 * HD), lambda g: (0, 0)),
        ),
        name="prepare",
    )(query_self, key_self, value_self, query_cross, key_vision, value_vision, cosine, sine, extra)

    span = heads // 2 * rows
    row = pltpu.VMEM((2 * ny, span), F32)
    state = pltpu.VMEM((2 * ny, HD, span), F32)
    part = pltpu.VMEM((ny, HD, heads * rows), BF16)
    stat = pltpu.VMEM((2, ny, 1, heads * rows), F32)
    final = pltpu.VMEM((nh, rows // nh, wide), BF16)
    dma = pltpu.SemaphoreType.DMA
    half = nz // 2
    return pl.pallas_call(
        functools.partial(main_kernel, nz, ny, nh, real, zpf),
        out_shape=(jax.ShapeDtypeStruct((rows // nh, wide * nh), BF16),) * 2,
        in_specs=[anywhere] * 3 + [vmem],
        out_specs=(vmem,) * 2,
        scratch_shapes=[
            pltpu.VMEM((nz, 2 * rows, 2 * HD), BF16),
            pltpu.VMEM((ny, rows, wide), BF16),
            pltpu.VMEM((ny, rows, wide + HD), BF16),
            pltpu.VMEM((ny, rows, HD), BF16),
            row, row, state, row, row, state,
            pltpu.VMEM((2, 4 * rows, span), F32),
            pltpu.VMEM((2, 2, HD, span), BF16),
            part, part, stat, part, part, stat, final, final,
            dma((2, half + 1, 2)), dma((2, half + 1, 2)),
            dma((2, ny)), dma((2, ny)),
            dma((4, ny)), dma((4, ny)),
            dma((2, 4)), dma((2, 4)),
            dma((2, nh)), dma((2, nh)),
            dma((5,)),
        ],
        compiler_params=pltpu.CompilerParams(collective_id=0, has_side_effects=True),
        name="attend",
    )(qs, qc, kv, gate)


def solution(mesh):
    placed = (
        P("ctx", "head"),
        P("ctx", "head"),
        P("ctx", "head"),
        P("ctx"),
        P("ctx", "head"),
        P("ctx", "head"),
        P("ctx", "head"),
        P("ctx", None),
        P(),
    )
    body = functools.partial(on_device, mesh.shape["ctx"], mesh.shape["head"])
    return jax.shard_map(
        body,
        mesh=mesh,
        in_specs=placed,
        out_specs=(P(("ctx", "head"), None), P(("ctx", "head"), None)),
        check_vma=False,
    )
```

```python
import functools
import math

import jax
import jax.numpy as jnp
from jax import lax
from jax.experimental import pallas as pl
from jax.experimental.pallas import tpu as pltpu
from jax.sharding import PartitionSpec as P

HD = 128
TBLOCK = 16
FRAME_LEN = 896
NY = 4
ROPE_BASE = 500000.0
BIG = 1e30
LOWEST = -3e38
LOG2 = HD ** -0.5 * math.log2(math.e)
MESH = pl.DeviceIdType.MESH
F32 = jnp.float32
BF16 = jnp.bfloat16


def prepare_kernel(qs, ks, vs, qc, kf, vf, cos, sin, qa, o_qs, o_qc, o_kv):
    rows = qs.shape[0]
    heads = qs.shape[1] // HD
    cosine = cos[...]
    sine = sin[...]

    def turned(x):
        x = x.astype(F32)
        return (x * cosine + pltpu.roll(x, HD // 2, 1) * sine).astype(BF16)

    o_kv[0:rows, 0:HD] = turned(ks[...])
    o_kv[0:rows, HD:] = vs[...]
    pad = jnp.zeros((rows - kf.shape[0], HD), F32)
    o_kv[rows:, 0:HD] = jnp.concatenate([kf[...].astype(F32), pad], 0).astype(BF16)
    o_kv[rows:, HD:] = jnp.concatenate([vf[...].astype(F32), pad], 0).astype(BF16)
    for h in range(heads):
        cut = slice(h * HD, (h + 1) * HD)
        o_qs[:, cut] = turned(qs[:, cut])
    o_qc[:, 0 : heads * HD] = qc[...]
    o_qc[:, heads * HD :] = qa[...]


def main_kernel(
    nz, ny, nh, real, zpf,
    qs, qc, kv, gate, out_s, out_c,
    kvb, qsb, qcb, qat, m_s, l_s, acc_s, m_c, l_c, acc_c,
    scb, rel, osb, ocb, stb, rsb, rcb, rst, fsb, fcb,
    r_ring, s_ring, r_q, s_q, r_o, s_o, r_r, s_r, r_f, s_f, loc,
):
    rows = qs.shape[0]
    wide = qs.shape[1]
    heads = wide // HD
    packed = heads // 2
    span = packed * rows
    half = nz // 2
    groups = nz // 4
    ctx = lax.axis_index("ctx")
    head = lax.axis_index("head")
    z = ctx // ny
    y = ctx % ny
    z_up = (z + 1) % nz
    z_dn = (z + nz - 1) % nz

    def at_z(other):
        return (other * ny + y, head)

    def at_y(i):
        return (z * ny + (y + i) % ny, head)

    def at_h(i):
        return (ctx, (head + i) % nh)

    def slot(offset):
        return (z + nz + offset) % nz

    def ring(flow, d, piece, first=False):
        at = slot(d - 1) if flow == 0 else slot(1 - d)
        part = pl.ds(piece * rows, rows)
        return pltpu.make_async_remote_copy(
            src_ref=kv.at[part, :] if first else kvb.at[at, part, :],
            dst_ref=kvb.at[at, part, :],
            send_sem=s_ring.at[flow, d, piece],
            recv_sem=r_ring.at[flow, d, piece],
            device_id=at_z(z_dn if flow == 0 else z_up),
            device_id_type=MESH,
        )

    def ring_in(flow, d, piece):
        at = slot(d) if flow == 0 else slot(-d)
        part = pl.ds(piece * rows, rows)
        return pltpu.make_async_remote_copy(
            src_ref=kvb.at[at, part, :],
            dst_ref=kvb.at[at, part, :],
            send_sem=s_ring.at[flow, d, piece],
            recv_sem=r_ring.at[flow, d, piece],
            device_id=at_z(z_dn if flow == 0 else z_up),
            device_id_type=MESH,
        )

    def q_copy(kind, i):
        src, dst = ((qs, qsb), (qc, qcb))[kind]
        return pltpu.make_async_remote_copy(
            src_ref=src,
            dst_ref=dst.at[ny - i],
            send_sem=s_q.at[kind, ny - i],
            recv_sem=r_q.at[kind, ny - i],
            device_id=at_y(i),
            device_id_type=MESH,
        )

    def q_relay(kind):
        dst = (qsb, qcb)[kind]
        came, goes = ((ny - 1, 1), (1, ny - 1))[kind]
        return pltpu.make_async_remote_copy(
            src_ref=dst.at[came],
            dst_ref=dst.at[2],
            send_sem=s_q.at[kind, 2],
            recv_sem=r_q.at[kind, 2],
            device_id=at_y(goes),
            device_id_type=MESH,
        )

    def o_copy(kind, i):
        src, dst = ((osb, rsb), (ocb, rcb))[kind]
        return pltpu.make_async_remote_copy(
            src_ref=src.at[i],
            dst_ref=dst.at[ny - i],
            send_sem=s_o.at[kind, ny - i],
            recv_sem=r_o.at[kind, ny - i],
            device_id=at_y(i),
            device_id_type=MESH,
        )

    def o_half(kind, j):
        src = (osb, ocb)[kind]
        return pltpu.make_async_remote_copy(
            src_ref=src.at[2, :, pl.ds(j * span, span)],
            dst_ref=rel.at[kind, j],
            send_sem=s_r.at[kind, j],
            recv_sem=r_r.at[kind, j],
            device_id=at_y((1, ny - 1)[j]),
            device_id_type=MESH,
        )

    def o_relay(kind, j):
        dst = (rsb, rcb)[kind]
        return pltpu.make_async_remote_copy(
            src_ref=rel.at[kind, j],
            dst_ref=dst.at[2, :, pl.ds(j * span, span)],
            send_sem=s_r.at[kind, 2 + j],
            recv_sem=r_r.at[kind, 2 + j],
            device_id=at_y((1, ny - 1)[j]),
            device_id_type=MESH,
        )

    def t_copy(kind, i):
        return pltpu.make_async_remote_copy(
            src_ref=stb.at[kind, i],
            dst_ref=rst.at[kind, ny - i],
            send_sem=s_o.at[2 + kind, ny - i],
            recv_sem=r_o.at[2 + kind, ny - i],
            device_id=at_y(i),
            device_id_type=MESH,
        )

    def f_copy(kind, i):
        src, dst = ((fsb, out_s), (fcb, out_c))[kind]
        return pltpu.make_async_remote_copy(
            src_ref=src.at[(head + i) % nh],
            dst_ref=dst.at[:, pl.ds(pl.multiple_of(head * wide, wide), wide)],
            send_sem=s_f.at[kind, i],
            recv_sem=r_f.at[kind, i],
            device_id=at_h(i),
            device_id_type=MESH,
        )

    def f_in(kind, i):
        src, dst = ((fsb, out_s), (fcb, out_c))[kind]
        other = (head + nh - i) % nh
        return pltpu.make_async_remote_copy(
            src_ref=src.at[other],
            dst_ref=dst.at[:, pl.ds(pl.multiple_of(other * wide, wide), wide)],
            send_sem=s_f.at[kind, i],
            recv_sem=r_f.at[kind, i],
            device_id=at_h(i),
            device_id_type=MESH,
        )

    own_kv = pltpu.make_async_copy(kv, kvb.at[z], loc.at[0])
    own_qs = pltpu.make_async_copy(qs, qsb.at[0], loc.at[1])
    own_qc = pltpu.make_async_copy(qc, qcb.at[0], loc.at[2])
    own_kv.start()
    own_qs.start()
    own_qc.start()

    barrier = pltpu.get_barrier_semaphore()
    partners = [at_z(z_up), at_z(z_dn)]
    partners += [at_y(i) for i in range(1, ny)]
    partners += [at_h(i) for i in range(1, nh)]
    for partner in partners:
        pl.semaphore_signal(barrier, inc=1, device_id=partner, device_id_type=MESH)
    pl.semaphore_wait(barrier, len(partners))

    for piece in range(2):
        ring(0, 1, piece, True).start()
        ring(1, 1, piece, True).start()
    for kind in range(2):
        for i in (1, ny - 1):
            q_copy(kind, i).start()

    lane = lax.broadcasted_iota(jnp.int32, (rows, HD), 1)
    token = lax.broadcasted_iota(jnp.int32, (rows, HD), 0)
    late = jnp.logical_and(lane < nz, lane > z)
    for i in range(ny):
        place = ((y + i) % ny - y) * rows + token
        ahead = jnp.logical_and(lane >= rows, lane - rows > place)
        qat[i] = jnp.where(jnp.logical_or(late, ahead), -BIG, 0.0).astype(BF16)
    for m_r, l_r in ((m_s, l_s), (m_c, l_c)):
        m_r[...] = jnp.full(m_r.shape, LOWEST, F32)
        l_r[...] = jnp.zeros(l_r.shape, F32)

    @pl.loop(0, 2 * ny)
    def _(b):
        acc_s[b] = jnp.zeros((HD, span), F32)
        acc_c[b] = jnp.zeros((HD, span), F32)

    own_kv.wait()
    own_qs.wait()
    own_qc.wait()

    def serve(d, piece):
        ring_in(0, d, piece).wait_recv()

        @pl.when(d < half)
        def _():
            ring(0, d + 1, piece).start()

        @pl.when(d < half)
        def _():
            ring_in(1, d, piece).wait_recv()

        @pl.when(d < half - 1)
        def _():
            ring(1, d + 1, piece).start()

    def keys_of(kind, group):
        offsets = (-2 * group, -2 * group - 1, 2 * group + 1, 2 * group + 2)
        keys, marks, values = [], [], []
        lanes = lax.broadcasted_iota(jnp.int32, (rows, HD), 1)
        index = lax.broadcasted_iota(jnp.int32, (rows, HD), 0)
        for offset in offsets:
            at = slot(offset)
            part = slice(kind * rows, (kind + 1) * rows)
            keys.append(kvb[at, part, 0:HD])
            values.append(kvb[at, part, HD:])
            if kind == 0:
                mark = jnp.where(at == z, rows + index, at)
            else:
                mark = jnp.where(index < real, at // zpf, HD - 1)
            marks.append(jnp.where(lanes == mark, 1.0, 0.0).astype(BF16))
        key = jnp.concatenate([jnp.concatenate(keys, 0), jnp.concatenate(marks, 0)], 1)
        value = jnp.concatenate(values, 0).astype(F32)
        return key, jnp.transpose(value).astype(BF16)

    def q_wait(kind, i):
        if i == 2:
            q_relay(kind).wait_recv()
        elif i > 0:
            q_copy(kind, ny - i).wait_recv()

    def attend(kind, group, sources):
        key, value = keys_of(kind, group)
        qb = (qsb, qcb)[kind]
        m_r, l_r, acc_r = ((m_s, l_s, acc_s), (m_c, l_c, acc_c))[kind]

        def score(i, j, turn):
            b = 2 * i + j
            extra = qat[i] if kind == 0 else qcb[i, :, wide:]
            parts = [
                qb[i, :, h * HD : (h + 1) * HD]
                for h in range(j * packed, (j + 1) * packed)
            ]
            q = jnp.concatenate(
                [jnp.concatenate(parts, 0), jnp.concatenate([extra] * packed, 0)], 1
            )
            scores = lax.dot_general(
                key, q, (((1,), (1,)), ((), ())), preferred_element_type=F32
            )
            scb[turn] = scores
            m_old = m_r[b : b + 1, :]
            m_new = jnp.maximum(m_old, jnp.max(scores, axis=0, keepdims=True))
            m_r[b : b + 1, :] = m_new
            return m_new, jnp.exp2((m_old - m_new) * LOG2)

        def fold(i, j, turn, m_new, alpha):
            b = 2 * i + j
            weights = jnp.exp2((scb[turn] - m_new) * LOG2)
            l_r[b : b + 1, :] = l_r[b : b + 1, :] * alpha + jnp.sum(
                weights, axis=0, keepdims=True
            )
            acc_r[b] = acc_r[b] * alpha + jnp.dot(
                value, weights.astype(BF16), preferred_element_type=F32
            )

        blocks = [(i, j) for i in sources for j in range(2)]
        held = score(*blocks[0], 0)
        for n, block in enumerate(blocks):
            coming = None
            if n + 1 < len(blocks):
                coming = score(*blocks[n + 1], (n + 1) % 2)
            fold(*block, n % 2, *held)
            held = coming

    def send_off(kind):
        m_r, l_r, acc_r = ((m_s, l_s, acc_s), (m_c, l_c, acc_c))[kind]
        dst = (osb, ocb)[kind]
        for i in (2, 1, ny - 1, 0):
            for j in range(2):
                b = 2 * i + j
                cut = slice(j * span, (j + 1) * span)
                total = l_r[b : b + 1, :]
                dst[i, :, cut] = (acc_r[b] / total).astype(BF16)
                stb[kind, i, :, cut] = m_r[b : b + 1, :] * LOG2 + jnp.log2(total)
        for j in range(2):
            o_half(kind, j).start()
        for i in range(1, ny):
            t_copy(kind, i).start()
        for i in (1, ny - 1):
            o_copy(kind, i).start()

    def pass_on(kind):
        for j in range(2):
            o_half(kind, j).wait_recv()
            o_relay(kind, j).start()

    low = (0, 1)
    high = (ny - 1, 2)

    @pl.loop(0, groups)
    def _(g):
        for turn in range(4):
            serve(2 * g + 1 + turn // 2, turn % 2)
            kind = turn // 2
            sources = (low, high)[turn % 2]
            if turn == 3:
                @pl.when(g == 0)
                def _():
                    q_wait(0, ny - 1)
                    q_relay(0).start()

            if turn == 1:
                @pl.when(g == 1)
                def _():
                    q_wait(1, 1)
                    q_relay(1).start()

            @pl.when(g == kind + 1)
            def _():
                for i in sources:
                    if i != (ny - 1, 1)[kind]:
                        q_wait(kind, i)

            behind = 1 if kind == 0 else jnp.where(g > 4, 1, 2)

            @pl.when(g > kind)
            def _():
                attend(kind, g - behind, sources)

            if kind == 1:
                @pl.when(g == 4)
                def _():
                    attend(kind, g - 1, sources)

    attend(0, groups - 1, low + high)
    send_off(0)
    attend(1, groups - 1, low + high)
    pass_on(0)
    send_off(1)

    for kind in range(2):
        mine, other = ((osb, rsb), (ocb, rcb))[kind]
        final, out = ((fsb, out_s), (fcb, out_c))[kind]
        for i in range(1, ny):
            t_copy(kind, ny - i).wait_recv()
        levels = [stb[kind, 0]] + [rst[kind, i] for i in range(1, ny)]
        top = levels[0]
        for level in levels[1:]:
            top = jnp.maximum(top, level)
        shares = [jnp.exp2(level - top) for level in levels]
        whole = shares[0]
        for share in shares[1:]:
            whole = whole + share
        shares = [share / whole for share in shares]
        for i in (1, ny - 1):
            o_copy(kind, ny - i).wait_recv()
        for j in range(2):
            o_relay(kind, j).wait_recv()
        for pair in range(heads // 2):
            cut = slice(pair * 2 * rows, (pair + 1) * 2 * rows)
            mixed = mine[0, :, cut].astype(F32) * shares[0][:, cut]
            for i in range(1, ny):
                mixed = mixed + other[i, :, cut].astype(F32) * shares[i][:, cut]
            mixed = jnp.transpose(mixed)
            for k in range(2):
                h = 2 * pair + k
                block = mixed[k * rows : (k + 1) * rows, :]
                if kind == 1:
                    block = block * gate[...]
                final[:, :, h * HD : (h + 1) * HD] = block.reshape(
                    nh, rows // nh, HD
                ).astype(BF16)
        for i in range(1, nh):
            f_copy(kind, i).start()
        if kind == 0:
            pass_on(1)
        pltpu.make_async_copy(
            final.at[head],
            out.at[:, pl.ds(pl.multiple_of(head * wide, wide), wide)],
            loc.at[3 + kind],
        ).start()
    for kind in range(2):
        final, out = ((fsb, out_s), (fcb, out_c))[kind]
        for i in range(1, nh):
            f_in(kind, i).wait_recv()
        pltpu.make_async_copy(
            final.at[head],
            out.at[:, pl.ds(pl.multiple_of(head * wide, wide), wide)],
            loc.at[3 + kind],
        ).wait()

    for piece in range(2):
        ring(0, 1, piece, True).wait_send()
        ring(1, 1, piece, True).wait_send()
        ring(0, half, piece).wait_send()

    @pl.loop(2, half)
    def _(d):
        for flow in range(2):
            for piece in range(2):
                ring(flow, d, piece).wait_send()

    for kind in range(2):
        for i in (1, ny - 1):
            q_copy(kind, i).wait_send()
            o_copy(kind, i).wait_send()
        q_relay(kind).wait_send()
        for i in range(1, ny):
            t_copy(kind, i).wait_send()
        for j in range(2):
            o_half(kind, j).wait_send()
            o_relay(kind, j).wait_send()
    for kind in range(2):
        for i in range(1, nh):
            f_copy(kind, i).wait_send()


def on_device(
    nctx, nh,
    query_self, key_self, value_self, positions,
    query_cross, key_vision, value_vision, media_range, gate_scale,
):
    rows, wide = query_self.shape
    real = key_vision.shape[0]
    ny = NY
    nz = nctx // ny
    heads = wide // HD
    zpf = FRAME_LEN // (real * ny)

    exponents = jnp.arange(HD // 2, dtype=F32) * (2.0 / HD)
    frequency = jnp.power(ROPE_BASE, -exponents)
    angles = positions.astype(F32)[:, None] * jnp.tile(frequency, 2)[None, :]
    first = jnp.arange(HD)[None, :] < HD // 2
    cosine = jnp.cos(angles)
    sine = jnp.where(first, -jnp.sin(angles), jnp.sin(angles))

    lower = jnp.repeat(media_range[:, 0], TBLOCK)[:, None]
    upper = jnp.repeat(media_range[:, 1], TBLOCK)[:, None]
    lanes = jnp.arange(HD, dtype=jnp.int32)[None, :]
    hidden = jnp.logical_or(lanes < lower, lanes >= upper)
    hidden = jnp.logical_and(hidden, lanes < nz // zpf)
    hidden = jnp.logical_or(hidden, lanes == HD - 1)
    extra = jnp.where(hidden, -BIG, 0.0).astype(BF16)
    gate = jnp.where(upper > lower, jnp.tanh(gate_scale[0]), 0.0)
    gate = jnp.broadcast_to(gate, (rows, HD)).astype(F32)

    vmem = pl.BlockSpec(memory_space=pltpu.VMEM)
    anywhere = pl.BlockSpec(memory_space=pl.ANY)
    qs, qc, kv = pl.pallas_call(
        prepare_kernel,
        out_shape=(
            jax.ShapeDtypeStruct((rows, wide), BF16),
            jax.ShapeDtypeStruct((rows, wide + HD), BF16),
            jax.ShapeDtypeStruct((2 * rows, 2 * HD), BF16),
        ),
        grid=(1,),
        in_specs=[vmem] * 9,
        out_specs=(
            pl.BlockSpec((rows, wide), lambda g: (0, 0)),
            pl.BlockSpec((rows, wide + HD), lambda g: (0, 0)),
            pl.BlockSpec((2 * rows, 2 * HD), lambda g: (0, 0)),
        ),
        name="prepare",
    )(query_self, key_self, value_self, query_cross, key_vision, value_vision, cosine, sine, extra)

    span = heads // 2 * rows
    row = pltpu.VMEM((2 * ny, span), F32)
    state = pltpu.VMEM((2 * ny, HD, span), F32)
    part = pltpu.VMEM((ny, HD, heads * rows), BF16)
    stat = pltpu.VMEM((2, ny, 1, heads * rows), F32)
    final = pltpu.VMEM((nh, rows // nh, wide), BF16)
    dma = pltpu.SemaphoreType.DMA
    half = nz // 2
    return pl.pallas_call(
        functools.partial(main_kernel, nz, ny, nh, real, zpf),
        out_shape=(jax.ShapeDtypeStruct((rows // nh, wide * nh), BF16),) * 2,
        in_specs=[anywhere] * 3 + [vmem],
        out_specs=(vmem,) * 2,
        scratch_shapes=[
            pltpu.VMEM((nz, 2 * rows, 2 * HD), BF16),
            pltpu.VMEM((ny, rows, wide), BF16),
            pltpu.VMEM((ny, rows, wide + HD), BF16),
            pltpu.VMEM((ny, rows, HD), BF16),
            row, row, state, row, row, state,
            pltpu.VMEM((2, 4 * rows, span), F32),
            pltpu.VMEM((2, 2, HD, span), BF16),
            part, part, stat, part, part, stat, final, final,
            dma((2, half + 1, 2)), dma((2, half + 1, 2)),
            dma((2, ny)), dma((2, ny)),
            dma((4, ny)), dma((4, ny)),
            dma((2, 4)), dma((2, 4)),
            dma((2, nh)), dma((2, nh)),
            dma((5,)),
        ],
        compiler_params=pltpu.CompilerParams(collective_id=0, has_side_effects=True),
        name="attend",
    )(qs, qc, kv, gate)


def solution(mesh):
    placed = (
        P("ctx", "head"),
        P("ctx", "head"),
        P("ctx", "head"),
        P("ctx"),
        P("ctx", "head"),
        P("ctx", "head"),
        P("ctx", "head"),
        P("ctx", None),
        P(),
    )
    body = functools.partial(on_device, mesh.shape["ctx"], mesh.shape["head"])
    return jax.shard_map(
        body,
        mesh=mesh,
        in_specs=placed,
        out_specs=(P(("ctx", "head"), None), P(("ctx", "head"), None)),
        check_vma=False,
    )
```
